512 devices in a mesh: slab: 128 (over x, z, y_hi), col: 4 (over y_lo, core).
Axes of the slice: x: 4, y: 4 (y_hi: 2, y_lo: 2; y = y_hi * 2 + y_lo), z: 16, core: 2. Of those that a mesh axis runs over, the one named last changes fastest.
Arguments:
- rhs: float32 [1024, 32, 384], P(('slab', 'col')), may hold values from -6 to 6
- tiles: bfloat16 [1024, 6, 384, 384], P(('slab', 'col'))
- neighbours: int32 [1024, 6], P(('slab', 'col')), may hold values from 0 to 1023, as said below
- smoother: bfloat16 [1024, 384, 384], P(('slab', 'col'))
- basis: bfloat16 [1024, 256, 384], P(('slab', 'col')), may hold values from -0.29882812 to 0.29882812
Outputs:
- solution: float32 [1024, 32, 384], P(('slab', 'col'))
- coarse_iterate: float32 [1024, 32, 256], P(('slab', 'col'))
The draws below stay inside these ranges and needn't reach their ends.
Inputs may be any that keep to these rules, and one draw needn't show every extreme that they name: `neighbours`: entry [g, 0] is g itself; every other entry names a cell whose slab (cell // 8) is the slab of g or one of the two beside it, counted around 128 slabs.
All inputs are finite; a program needn't handle non-finite values.
Results may differ from the reference program's by a relative error of at most 0.0023.
The reference program's roundings to bfloat16 on the way count: a program that leaves them out, or rounds other values in their place, can miss the bound.
Values may be sent and summed in bfloat16 or wider, within the bound.
No kernel may reach another device: no remote copies, remote signals or barrier semaphores. Data moves between devices by JAX's collectives and lax.ppermute only.
A program may use at most 128 MiB of HBM per device.

```python
import jax
import jax.numpy as jnp
from jax import lax

BLOCK = 384
COARSE = 256
NRHS = 32
NB = 6
SLAB_CELLS = 8
SLABS = 128
CELLS = 1024


def draw_tiles(key, part):
    key_noise = jax.random.fold_in(key, 101)
    key_diag = jax.random.fold_in(key, 102)
    noise = jnp.clip(jax.random.normal(key_noise, (CELLS, NB, BLOCK, BLOCK), jnp.float32) * 0.03, -0.12, 0.12)
    diag = jax.random.uniform(key_diag, (CELLS, BLOCK), jnp.float32, 2.0, 4.0)
    own = noise[:, 0]
    symmetric = (own + jnp.swapaxes(own, 1, 2)) * 0.7071
    identity = jnp.eye(BLOCK, dtype=jnp.float32)
    own_tile = symmetric + identity[None, :, :] * diag[:, :, None]
    full = noise.at[:, 0].set(own_tile)
    return full.astype(jnp.bfloat16)


def draw_smoother(key, part):
    key_noise = jax.random.fold_in(key, 201)
    key_diag = jax.random.fold_in(key, 202)
    noise = jnp.clip(jax.random.normal(key_noise, (CELLS, BLOCK, BLOCK), jnp.float32) * 0.01, -0.04, 0.04)
    diag = jax.random.uniform(key_diag, (CELLS, BLOCK), jnp.float32, 0.25, 0.45)
    identity = jnp.eye(BLOCK, dtype=jnp.float32)
    return (noise + identity[None, :, :] * diag[:, :, None]).astype(jnp.bfloat16)


def draw_neighbours(key, part):
    key_step = jax.random.fold_in(key, 301)
    key_place = jax.random.fold_in(key, 302)
    step = jax.random.randint(key_step, (CELLS, NB), -1, 2)
    place = jax.random.randint(key_place, (CELLS, NB), 0, SLAB_CELLS)
    cell_ids = jnp.arange(CELLS, dtype=jnp.int32)
    home_slab = cell_ids // SLAB_CELLS
    other = (home_slab[:, None] + step + SLABS) % SLABS * SLAB_CELLS + place
    other = other.at[:, 0].set(cell_ids)
    return other.astype(jnp.int32)


def steps_of(key, shape, pieces, least, high):
    def one(dim, parts):
        steps = jax.random.uniform(jax.random.fold_in(jax.random.fold_in(key, 6), dim), (parts,), jnp.float32, least / len(pieces), high / len(pieces))
        return jnp.repeat(jnp.exp(steps), shape[dim] // parts).reshape((-1,) + (1,) * (len(shape) - dim - 1))

    factor_of = one(*pieces[0])
    for cut in pieces[1:]:
        factor_of = factor_of * one(*cut)
    return factor_of


def gaussian(key, shape, width, most, cuts=(), held_as=jnp.bfloat16):
    entries = width * jax.random.normal(key, shape, jnp.float32)
    if cuts:
        entries = entries * steps_of(key, shape, cuts, -0.22, 0.18)
    return jnp.clip(entries, -most, most).astype(held_as)


def setup_inputs(seed: int = 0) -> dict:
    seeds = jax.random.split(jax.random.key(seed), 6)
    rhs = gaussian(seeds[0], (CELLS, NRHS, BLOCK), 1.0, 6.0, ((0, 512),), jnp.float32)
    tiles = draw_tiles(jax.random.fold_in(seeds[5], 71), 0)
    neighbours = draw_neighbours(jax.random.fold_in(seeds[5], 71), 0)
    smoother = draw_smoother(jax.random.fold_in(seeds[5], 71), 0)
    basis = gaussian(seeds[4], (CELLS, COARSE, BLOCK), 0.05, 0.29882812, ((0, 512),))
    return dict(rhs=rhs, tiles=tiles, neighbours=neighbours, smoother=smoother, basis=basis)


damping = 0.8


def rounded(value):
    return lax.optimization_barrier(value.astype(jnp.bfloat16)).astype(jnp.float32)


def reference(rhs, tiles, neighbours, smoother, basis):
    def fine_apply(vec_rounded):
        def one_row(item):
            tile_row, index = item
            near = vec_rounded[index]
            return jnp.einsum('tri,tio->ro', near, tile_row.astype(jnp.float32))
        return lax.map(one_row, (tiles, neighbours))

    def smooth(residue):
        return jnp.einsum('gri,gio->gro', rounded(residue), smoother.astype(jnp.float32))

    x_first = smooth(rhs)
    x_second = x_first + smooth(rhs - fine_apply(rounded(x_first)))
    fine_residual = rhs - fine_apply(rounded(x_second))

    def coarse_row(item):
        tile_row, index, own = item
        near = basis[index].astype(jnp.float32)
        upper = rounded(jnp.einsum('tci,tio->tco', near, tile_row.astype(jnp.float32)))
        return jnp.einsum('tco,do->tcd', upper, own.astype(jnp.float32)).astype(jnp.bfloat16)

    coarse_tiles = lax.map(coarse_row, (tiles, neighbours, basis))
    pivots = jnp.diagonal(coarse_tiles[:, 0].astype(jnp.float32), axis1=1, axis2=2)
    coarse_rhs = jnp.einsum('gri,gci->grc', rounded(fine_residual), basis.astype(jnp.float32))

    def coarse_apply(vec_rounded):
        def one_row(item):
            tile_row, index = item
            near = vec_rounded[index]
            return jnp.einsum('trc,tcd->rd', near, tile_row.astype(jnp.float32))
        return lax.map(one_row, (coarse_tiles, neighbours))

    c_first = damping * coarse_rhs / pivots[:, None, :]
    coarse_iterate = c_first + damping * (coarse_rhs - coarse_apply(rounded(c_first))) / pivots[:, None, :]
    solution = x_second + jnp.einsum('grc,gci->gri', rounded(coarse_iterate), basis.astype(jnp.float32))
    return solution, coarse_iterate
```

```python
import functools

import jax
import jax.numpy as jnp
from jax import lax
from jax.experimental import pallas as pl
from jax.experimental.pallas import tpu as pltpu
from jax.sharding import PartitionSpec as P

damping = 0.8
AXES = ("slab", "col")
VMEM = pltpu.VMEM
bf16 = jnp.bfloat16
f32 = jnp.float32


def dot(a, b):
    return jnp.dot(a, b, preferred_element_type=f32)


def dot_t(a, b):
    return lax.dot_general(a, b, (((1,), (1,)), ((), ())), preferred_element_type=f32)


def split(value):
    high = value.astype(bf16)
    return high, (value - high.astype(f32)).astype(bf16)


def pairs(slabs, cols, partner):
    groups = []
    for s in range(slabs):
        for c in range(cols):
            s2, c2 = partner(s, c)
            i, j = s * cols + c, (s2 % slabs) * cols + c2
            if i < j:
                groups.append([i, j])
    return groups


def exchange(cells, slabs, cols):
    def crossing(s, c):
        even = s % 2 == 0
        up = even == (c % 2 == 0)
        return (s + 1 if up else s - 1), c ^ 2

    def send(s, c):
        s2, c2 = crossing(s, c)
        return s * cols + c, (s2 % slabs) * cols + c2

    own = lax.all_gather(cells, "col", axis=0, tiled=True)
    beside = lax.ppermute(
        own, AXES, [send(s, c) for s in range(slabs) for c in range(cols)]
    )
    halo = lax.all_gather(
        beside,
        AXES,
        axis=0,
        tiled=True,
        axis_index_groups=pairs(slabs, cols, lambda s, c: (s, c ^ 1)),
    )
    return own, halo


def pick(own, halo, cell, here, slab_cells):
    slab = lax.div(cell, slab_cells)
    offset = lax.rem(cell, slab_cells)
    inside = lax.div(slab, 2) == lax.div(here, 2)
    there = halo[jnp.where(inside, offset, slab_cells + offset)]
    return jnp.where(slab == here, own[offset], there)


def fetch(tiles_hbm, tiles, sems, first=0):
    copies = {}
    for t in range(first, tiles.shape[1]):
        for g in range(tiles.shape[0]):
            copies[g, t] = pltpu.make_async_copy(
                tiles_hbm.at[g, t], tiles.at[g, t], sems.at[g, t]
            )
            copies[g, t].start()
    return copies


def apply_tiles(own, halo, nb, tiles, copies, slab_cells, first=0):
    here = lax.axis_index("slab")
    cells, kinds = tiles.shape[0], tiles.shape[1]
    sums = [None] * cells
    for t in range(first, kinds):
        for g in range(cells):
            copies[g, t].wait()
            part = dot(pick(own, halo, nb[g, t], here, slab_cells), tiles[g, t])
            sums[g] = part if sums[g] is None else sums[g] + part
    return sums


def first_body(rhs, own_tiles, smoother, basis, x_out, xb_out, coarse_out, pivot_out):
    for g in range(rhs.shape[0]):
        x = dot(rhs[g].astype(bf16), smoother[g])
        x_out[g] = x
        xb_out[g] = x.astype(bf16)
    size = basis.shape[1]
    eye = lax.broadcasted_iota(jnp.int32, (size, size), 0) == lax.broadcasted_iota(
        jnp.int32, (size, size), 1
    )
    for g in range(rhs.shape[0]):
        upper = dot(basis[g], own_tiles[g, 0]).astype(bf16)
        coarse = dot_t(upper, basis[g]).astype(bf16)
        coarse_out[g] = coarse
        pivot_out[g] = jnp.sum(
            jnp.where(eye, coarse.astype(f32), 0.0), axis=0, keepdims=True
        )


def second_body(slab_cells, nb, mine, halo, rhs, x_first, smoother, tiles_hbm, x_out, xb_out, tiles, sems):
    copies = fetch(tiles_hbm, tiles, sems)
    sums = apply_tiles(mine, halo, nb, tiles, copies, slab_cells)
    for g, image in enumerate(sums):
        x = x_first[g] + dot((rhs[g] - image).astype(bf16), smoother[g])
        x_out[g] = x
        xb_out[g] = x.astype(bf16)


def third_body(
    slab_cells, nb, mine, halo, rhs, basis, coarse, pivot, tiles_hbm, base_out, fine_out, tiles, sems
):
    copies = fetch(tiles_hbm, tiles, sems)
    sums = apply_tiles(mine, halo, nb, tiles, copies, slab_cells)
    rows = rhs.shape[1]
    for g, image in enumerate(sums):
        coarse_rhs = dot_t((rhs[g] - image).astype(bf16), basis[g])
        c_first = damping * coarse_rhs / pivot[g]
        rounded = c_first.astype(bf16)
        own = dot(rounded, coarse[g])
        base_out[g] = c_first + damping * (coarse_rhs - own) / pivot[g]
        high, low = split(dot(rounded, basis[g]))
        fine_out[g, :rows] = high
        fine_out[g, rows:] = low


def fourth_body(
    slab_cells, nb, mine, halo, base, x_second, basis, pivot, tiles_hbm, sol_out, iter_out, tiles, sems
):
    copies = fetch(tiles_hbm, tiles, sems, 1)
    sums = apply_tiles(mine, halo, nb, tiles, copies, slab_cells, 1)
    rows = x_second.shape[1]
    for g, image in enumerate(sums):
        high, low = split(image[:rows] + image[rows:])
        rest = dot_t(high, basis[g]) + dot_t(low, basis[g])
        iterate = base[g] - damping * rest / pivot[g]
        iter_out[g] = iterate
        sol_out[g] = x_second[g] + dot(iterate.astype(bf16), basis[g])


def call(body, outs, specs, scratch=()):
    return pl.pallas_call(
        body,
        out_shape=outs,
        in_specs=specs,
        out_specs=tuple(pl.BlockSpec(memory_space=VMEM) for _ in outs),
        scratch_shapes=list(scratch),
        compiler_params=pltpu.CompilerParams(vmem_limit_bytes=24 * 2**20),
    )


def per_device(slabs, cols, rhs, tiles, neighbours, smoother, basis):
    cells, rows, block = rhs.shape
    kinds, size = tiles.shape[1], basis.shape[1]
    slab_cells = cells * cols
    shape = jax.ShapeDtypeStruct
    vmem = pl.BlockSpec(memory_space=VMEM)
    smem = pl.BlockSpec(memory_space=pltpu.SMEM)
    anywhere = pl.BlockSpec(memory_space=pl.ANY)
    held = (
        pltpu.VMEM((cells, kinds, block, block), bf16),
        pltpu.SemaphoreType.DMA((cells, kinds)),
    )
    x_first, send, coarse, pivot = pl.pallas_call(
        first_body,
        grid=(1,),
        out_shape=(
            shape((cells, rows, block), f32),
            shape((cells, rows, block), bf16),
            shape((cells, size, size), bf16),
            shape((cells, 1, size), f32),
        ),
        in_specs=[
            vmem,
            pl.BlockSpec((cells, 1, block, block), lambda i: (0, 0, 0, 0)),
            vmem,
            vmem,
        ],
        out_specs=(vmem, vmem, vmem, vmem),
        compiler_params=pltpu.CompilerParams(vmem_limit_bytes=24 * 2**20),
    )(rhs, tiles, smoother, basis)
    near = exchange(send, slabs, cols)
    x_second, send = call(
        functools.partial(second_body, slab_cells),
        (shape((cells, rows, block), f32), shape((cells, rows, block), bf16)),
        [smem, vmem, vmem, vmem, vmem, vmem, anywhere],
        held,
    )(neighbours, *near, rhs, x_first, smoother, tiles)
    near = exchange(send, slabs, cols)
    base, send = call(
        functools.partial(third_body, slab_cells),
        (shape((cells, rows, size), f32), shape((cells, 2 * rows, block), bf16)),
        [smem, vmem, vmem, vmem, vmem, vmem, vmem, anywhere],
        held,
    )(neighbours, *near, rhs, basis, coarse, pivot, tiles)
    near = exchange(send, slabs, cols)
    return call(
        functools.partial(fourth_body, slab_cells),
        (shape((cells, rows, block), f32), shape((cells, rows, size), f32)),
        [smem, vmem, vmem, vmem, vmem, vmem, vmem, anywhere],
        held,
    )(neighbours, *near, base, x_second, basis, pivot, tiles)


def solution(mesh):
    placed = (
        P(AXES, None, None),
        P(AXES, None, None, None),
        P(AXES, None),
        P(AXES, None, None),
        P(AXES, None, None),
    )
    return jax.shard_map(
        functools.partial(per_device, mesh.shape["slab"], mesh.shape["col"]),
        mesh=mesh,
        in_specs=placed,
        out_specs=(P(AXES, None, None), P(AXES, None, None)),
        check_vma=False,
    )
```

```python
import functools

import jax
import jax.numpy as jnp
from jax import lax
from jax.experimental import pallas as pl
from jax.experimental.pallas import tpu as pltpu
from jax.sharding import PartitionSpec as P

damping = 0.8
AXES = ("slab", "col")
VMEM = pltpu.VMEM
bf16 = jnp.bfloat16
f32 = jnp.float32


def dot(a, b):
    return jnp.dot(a, b, preferred_element_type=f32)


def dot_t(a, b):
    return lax.dot_general(a, b, (((1,), (1,)), ((), ())), preferred_element_type=f32)


def split(value):
    high = value.astype(bf16)
    return high, (value - high.astype(f32)).astype(bf16)


def pairs(slabs, cols, partner):
    groups = []
    for s in range(slabs):
        for c in range(cols):
            s2, c2 = partner(s, c)
            i, j = s * cols + c, (s2 % slabs) * cols + c2
            if i < j:
                groups.append([i, j])
    return groups


def gather(values, slabs, cols, flip):
    return lax.all_gather(
        values,
        AXES,
        axis=0,
        tiled=True,
        axis_index_groups=pairs(slabs, cols, lambda s, c: (s, c ^ flip)),
    )


def crossing(s, c, slabs):
    up = (s % 2 == 0) == (c % 2 == 0)
    return (s + 1 if up else s - 1) % slabs, c ^ 2


def cross(values, slabs, cols):
    def target(s, c):
        s2, c2 = crossing(s, c, slabs)
        return s2 * cols + c2

    return lax.ppermute(
        values,
        AXES,
        [(s * cols + c, target(s, c)) for s in range(slabs) for c in range(cols)],
    )


def exchange(cells, slabs, cols):
    chip = gather(cells, slabs, cols, 1)
    beside = cross(chip, slabs, cols)
    own = gather(chip, slabs, cols, 2)
    return own, lax.all_gather(beside, "col", axis=0, tiled=True)


def pick(near, cell, here, slab_cells):
    slab = lax.div(cell, slab_cells)
    offset = lax.rem(cell, slab_cells)
    half = slab_cells // 2
    chip, inner = lax.div(offset, half), lax.rem(offset, half)
    odd = jnp.where(lax.div(slab, 2) == lax.div(here, 2), 0, 1)
    col = 2 * (1 - chip) + odd
    own, halo = near
    return jnp.where(slab == here, own[offset], halo[col * half + inner])


def apply_tiles(near, nb, tiles, slab_cells, first=0):
    here = lax.axis_index("slab")
    cells, kinds = tiles.shape[0], tiles.shape[1]
    sums = [None] * cells
    for t in range(first, kinds):
        for g in range(cells):
            part = dot(pick(near, nb[g, t], here, slab_cells), tiles[g, t])
            sums[g] = part if sums[g] is None else sums[g] + part
    return sums


def first_body(*refs):
    sources, (x_out, xb_out, rhs, smoother, basis, tiles), sems = refs[:4], refs[4:10], refs[10]
    copies = []
    for k, (source, target) in enumerate(zip(sources, (smoother, rhs, tiles, basis))):
        for g in range(rhs.shape[0]):
            copy = pltpu.make_async_copy(source.at[g], target.at[g], sems.at[k, g])
            copy.start()
            copies.append(copy)
    for copy in copies[: 2 * rhs.shape[0]]:
        copy.wait()
    for g in range(rhs.shape[0]):
        x = dot(rhs[g].astype(bf16), smoother[g])
        x_out[g] = x
        xb_out[g] = x.astype(bf16)
    for copy in copies[2 * rhs.shape[0] :]:
        copy.wait()


def coarse_body(own_tiles, basis, coarse_out, pivot_out):
    size = basis.shape[1]
    eye = lax.broadcasted_iota(jnp.int32, (size, size), 0) == lax.broadcasted_iota(
        jnp.int32, (size, size), 1
    )
    for g in range(basis.shape[0]):
        upper = dot(basis[g], own_tiles[g, 0]).astype(bf16)
        coarse = dot_t(upper, basis[g]).astype(bf16)
        coarse_out[g] = coarse
        pivot_out[g] = jnp.sum(
            jnp.where(eye, coarse.astype(f32), 0.0), axis=0, keepdims=True
        )


def second_body(slab_cells, nb, rhs, x_first, smoother, tiles, *refs):
    *near, x_out, xb_out = refs
    sums = apply_tiles(near, nb, tiles, slab_cells)
    for g, image in enumerate(sums):
        x = x_first[g] + dot((rhs[g] - image).astype(bf16), smoother[g])
        x_out[g] = x
        xb_out[g] = x.astype(bf16)


def third_body(
    slab_cells, nb, rhs, basis, coarse, pivot, tiles, *refs
):
    *near, base_out, fine_out = refs
    sums = apply_tiles(near, nb, tiles, slab_cells)
    rows = rhs.shape[1]
    for g, image in enumerate(sums):
        coarse_rhs = dot_t((rhs[g] - image).astype(bf16), basis[g])
        c_first = damping * coarse_rhs / pivot[g]
        rounded = c_first.astype(bf16)
        own = dot(rounded, coarse[g])
        base_out[g] = c_first + damping * (coarse_rhs - own) / pivot[g]
        high, low = split(dot(rounded, basis[g]))
        fine_out[g, :rows] = high
        fine_out[g, rows:] = low


def fourth_body(
    slab_cells, nb, base, x_second, basis, pivot, tiles, *refs
):
    *near, sol_out, iter_out = refs
    sums = apply_tiles(near, nb, tiles, slab_cells, 1)
    rows = x_second.shape[1]
    for g, image in enumerate(sums):
        parts = jnp.concatenate(split(image[:rows] + image[rows:]))
        both = dot_t(parts, basis[g])
        rest = both[:rows] + both[rows:]
        iterate = base[g] - damping * rest / pivot[g]
        iter_out[g] = iterate
        sol_out[g] = x_second[g] + dot(iterate.astype(bf16), basis[g])


def call(body, outs, specs, scratch=(), limit=24 * 2**20, moved=None):
    return pl.pallas_call(
        body,
        out_shape=outs,
        in_specs=specs,
        out_specs=tuple(pl.BlockSpec(memory_space=VMEM) for _ in outs),
        scratch_shapes=list(scratch),
        compiler_params=pltpu.CompilerParams(vmem_limit_bytes=limit),
        cost_estimate=moved
        and pl.CostEstimate(flops=0, transcendentals=0, bytes_accessed=moved),
    )


def per_device(slabs, cols, rhs, tiles, neighbours, smoother, basis):
    cells, rows, block = rhs.shape
    size = basis.shape[1]
    slab_cells = cells * cols
    shape = jax.ShapeDtypeStruct
    vmem = pl.BlockSpec(memory_space=VMEM)
    hbm = pl.BlockSpec(memory_space=pltpu.HBM)
    smem = pl.BlockSpec(memory_space=pltpu.SMEM)
    fixed = [
        pltpu.with_memory_space_constraint(v, pltpu.HBM) for v in (smoother, rhs, tiles, basis)
    ]
    x_first, send, rhs, smoother, basis, tiles = call(
        first_body,
        (shape((cells, rows, block), f32), shape((cells, rows, block), bf16))
        + tuple(shape(v.shape, v.dtype) for v in (rhs, smoother, basis, tiles)),
        [hbm] * 4,
        [pltpu.SemaphoreType.DMA((4, cells))],
    )(*fixed)
    coarse, pivot = call(
        coarse_body,
        (shape((cells, size, size), bf16), shape((cells, 1, size), f32)),
        [vmem, vmem],
    )(tiles, basis)
    near = exchange(send, slabs, cols)
    near, coarse, pivot = lax.optimization_barrier((near, coarse, pivot))
    x_second, send = call(
        functools.partial(second_body, slab_cells),
        (shape((cells, rows, block), f32), shape((cells, rows, block), bf16)),
        [smem] + [vmem] * (4 + len(near)),
    )(neighbours, rhs, x_first, smoother, tiles, *near)
    near = exchange(send, slabs, cols)
    base, send = call(
        functools.partial(third_body, slab_cells),
        (shape((cells, rows, size), f32), shape((cells, 2 * rows, block), bf16)),
        [smem] + [vmem] * (5 + len(near)),
    )(neighbours, rhs, basis, coarse, pivot, tiles, *near)
    near = exchange(send, slabs, cols)
    return call(
        functools.partial(fourth_body, slab_cells),
        (shape((cells, rows, block), f32), shape((cells, rows, size), f32)),
        [smem] + [vmem] * (5 + len(near)),
    )(neighbours, base, x_second, basis, pivot, tiles, *near)


def solution(mesh):
    placed = (
        P(AXES, None, None),
        P(AXES, None, None, None),
        P(AXES, None),
        P(AXES, None, None),
        P(AXES, None, None),
    )
    return jax.shard_map(
        functools.partial(per_device, mesh.shape["slab"], mesh.shape["col"]),
        mesh=mesh,
        in_specs=placed,
        out_specs=(P(AXES, None, None), P(AXES, None, None)),
        check_vma=False,
    )
```

```python
import functools

import jax
import jax.numpy as jnp
from jax import lax
from jax.experimental import pallas as pl
from jax.experimental.pallas import tpu as pltpu
from jax.sharding import PartitionSpec as P

damping = 0.8
AXES = ("slab", "col")
VMEM = pltpu.VMEM
bf16 = jnp.bfloat16
f32 = jnp.float32


def dot(a, b):
    return jnp.dot(a, b, preferred_element_type=f32)


def dot_t(a, b):
    return lax.dot_general(a, b, (((1,), (1,)), ((), ())), preferred_element_type=f32)


def split(value):
    high = value.astype(bf16)
    return high, (value - high.astype(f32)).astype(bf16)


def pairs(slabs, cols, partner):
    groups = []
    for s in range(slabs):
        for c in range(cols):
            s2, c2 = partner(s, c)
            i, j = s * cols + c, (s2 % slabs) * cols + c2
            if i < j:
                groups.append([i, j])
    return groups


def gather(values, slabs, cols, flip):
    return lax.all_gather(
        values,
        AXES,
        axis=0,
        tiled=True,
        axis_index_groups=pairs(slabs, cols, lambda s, c: (s, c ^ flip)),
    )


def crossing(s, c, slabs):
    up = (s % 2 == 0) == (c % 2 == 0)
    return (s + 1 if up else s - 1) % slabs, c ^ 2


def cross(values, slabs, cols):
    def target(s, c):
        s2, c2 = crossing(s, c, slabs)
        return s2 * cols + c2

    return lax.ppermute(
        values,
        AXES,
        [(s * cols + c, target(s, c)) for s in range(slabs) for c in range(cols)],
    )


def cross_now(values, slabs, cols):
    return lax.all_gather(
        values,
        AXES,
        axis=0,
        tiled=True,
        axis_index_groups=pairs(slabs, cols, lambda s, c: crossing(s, c, slabs)),
    )


def merge_body(slabs, cells, beside, out):
    n, extra = cells.shape[0], out.shape[0] - cells.shape[0]
    first = 0
    if beside.shape[0] != extra:
        s, c = lax.axis_index("slab"), lax.axis_index("col")
        up = lax.rem(s, 2) == lax.rem(c, 2)
        other = lax.rem(jnp.where(up, s + 1, s - 1 + slabs), slabs)
        first = jnp.where(s < other, extra, 0)
    for i in range(n):
        out[i] = cells[i]
    for i in range(extra):
        out[n + i] = beside[first + i]


def joined_exchange(cells, slabs, cols, move):
    chip = gather(cells, slabs, cols, 1)
    beside = move(chip, slabs, cols)
    total = (cells.shape[0] + chip.shape[0],) + cells.shape[1:]
    (joined,) = call(
        functools.partial(merge_body, slabs),
        (jax.ShapeDtypeStruct(total, cells.dtype),),
        [pl.BlockSpec(memory_space=VMEM)] * 2,
    )(cells, beside)
    return (lax.all_gather(joined, "col", axis=0, tiled=True),)


def exchange_apart(cells, slabs, cols):
    chip = gather(cells, slabs, cols, 1)
    beside = cross(chip, slabs, cols)
    own = gather(chip, slabs, cols, 2)
    return own, lax.all_gather(beside, "col", axis=0, tiled=True)


def pick(near, cell, here, slab_cells, cells):
    slab = lax.div(cell, slab_cells)
    offset = lax.rem(cell, slab_cells)
    half = slab_cells // 2
    chip, inner = lax.div(offset, half), lax.rem(offset, half)
    odd = jnp.where(lax.div(slab, 2) == lax.div(here, 2), 0, 1)
    col = 2 * (1 - chip) + odd
    if len(near) == 1:
        stride = half + cells
        mine = lax.div(offset, cells) * stride + lax.rem(offset, cells)
        return near[0][jnp.where(slab == here, mine, col * stride + cells + inner)]
    own, halo = near
    return jnp.where(slab == here, own[offset], halo[col * half + inner])


def apply_tiles(near, nb, tiles, slab_cells, first=0):
    here = lax.axis_index("slab")
    cells, kinds = tiles.shape[0], tiles.shape[1]
    sums = [None] * cells
    for t in range(first, kinds):
        for g in range(cells):
            part = dot(pick(near, nb[g, t], here, slab_cells, cells), tiles[g, t])
            sums[g] = part if sums[g] is None else sums[g] + part
    return sums


def load(source, target, sems):
    copies = []
    for g in range(target.shape[0]):
        copies.append(pltpu.make_async_copy(source.at[g], target.at[g], sems.at[g]))
        copies[-1].start()
    return copies


def first_body(smoother_hbm, rhs_hbm, x_out, xb_out, smoother, rhs, smoother_sems, rhs_sems):
    copies = zip(
        load(smoother_hbm, smoother, smoother_sems), load(rhs_hbm, rhs, rhs_sems)
    )
    for g, pair in enumerate(copies):
        for copy in pair:
            copy.wait()
        x = dot(rhs[g].astype(bf16), smoother[g])
        x_out[g] = x
        xb_out[g] = x.astype(bf16)


def coarse_body(
    tiles_hbm, basis_hbm, tiles, basis, coarse_out, pivot_out, own_sems, basis_sems, rest_sems
):
    cells, kinds = tiles.shape[0], tiles.shape[1]
    basis_copies = load(basis_hbm, basis, basis_sems)
    parts = [
        [
            pltpu.make_async_copy(
                tiles_hbm.at[g, pl.ds(first, count)],
                tiles.at[g, pl.ds(first, count)],
                sems.at[g],
            )
            for g in range(cells)
        ]
        for first, count, sems in ((0, 1, own_sems), (1, kinds - 1, rest_sems))
    ]
    for part in parts:
        for copy in part:
            copy.start()
    size = basis.shape[1]
    eye = lax.broadcasted_iota(jnp.int32, (size, size), 0) == lax.broadcasted_iota(
        jnp.int32, (size, size), 1
    )
    for g in range(cells):
        basis_copies[g].wait()
        parts[0][g].wait()
        upper = dot(basis[g], tiles[g, 0]).astype(bf16)
        coarse = dot_t(upper, basis[g]).astype(bf16)
        coarse_out[g] = coarse
        pivot_out[g] = jnp.sum(
            jnp.where(eye, coarse.astype(f32), 0.0), axis=0, keepdims=True
        )
    for copy in parts[1]:
        copy.wait()


def second_body(slab_cells, nb, rhs, x_first, smoother, tiles, *refs):
    *near, x_out, xb_out = refs
    sums = apply_tiles(near, nb, tiles, slab_cells)
    for g, image in enumerate(sums):
        x = x_first[g] + dot((rhs[g] - image).astype(bf16), smoother[g])
        x_out[g] = x
        xb_out[g] = x.astype(bf16)


def third_body(
    slab_cells, nb, rhs, basis, coarse, pivot, tiles, *refs
):
    *near, base_out, fine_out = refs
    sums = apply_tiles(near, nb, tiles, slab_cells)
    rows = rhs.shape[1]
    for g, image in enumerate(sums):
        coarse_rhs = dot_t((rhs[g] - image).astype(bf16), basis[g])
        c_first = damping * coarse_rhs / pivot[g]
        rounded = c_first.astype(bf16)
        own = dot(rounded, coarse[g])
        base_out[g] = c_first + damping * (coarse_rhs - own) / pivot[g]
        high, low = split(dot(rounded, basis[g]))
        fine_out[g, :rows] = high
        fine_out[g, rows:] = low


def fourth_body(
    slab_cells, nb, base, x_second, basis, pivot, tiles, *refs
):
    *near, sol_out, iter_out = refs
    sums = apply_tiles(near, nb, tiles, slab_cells, 1)
    rows = x_second.shape[1]
    for g, image in enumerate(sums):
        parts = jnp.concatenate(split(image[:rows] + image[rows:]))
        both = dot_t(parts, basis[g])
        rest = both[:rows] + both[rows:]
        iterate = base[g] - damping * rest / pivot[g]
        iter_out[g] = iterate
        sol_out[g] = x_second[g] + dot(iterate.astype(bf16), basis[g])


def call(body, outs, specs, scratch=(), limit=24 * 2**20, moved=None):
    return pl.pallas_call(
        body,
        out_shape=outs,
        in_specs=specs,
        out_specs=tuple(pl.BlockSpec(memory_space=VMEM) for _ in outs),
        scratch_shapes=list(scratch),
        compiler_params=pltpu.CompilerParams(vmem_limit_bytes=limit),
        cost_estimate=moved
        and pl.CostEstimate(flops=0, transcendentals=0, bytes_accessed=moved),
    )


def per_device(slabs, cols, rhs, tiles, neighbours, smoother, basis):
    cells, rows, block = rhs.shape
    size = basis.shape[1]
    slab_cells = cells * cols
    shape = jax.ShapeDtypeStruct
    vmem = pl.BlockSpec(memory_space=VMEM)
    hbm = pl.BlockSpec(memory_space=pltpu.HBM)
    smem = pl.BlockSpec(memory_space=pltpu.SMEM)
    fixed = [
        pltpu.with_memory_space_constraint(v, pltpu.HBM) for v in (smoother, rhs, tiles, basis)
    ]
    sems = pltpu.SemaphoreType.DMA((cells,))
    x_first, send, smoother, rhs = call(
        first_body,
        (
            shape((cells, rows, block), f32),
            shape((cells, rows, block), bf16),
            shape(smoother.shape, bf16),
            shape(rhs.shape, f32),
        ),
        [hbm] * 2,
        [sems] * 2,
    )(*fixed[:2])
    tiles, basis, coarse, pivot = call(
        coarse_body,
        (
            shape(tiles.shape, bf16),
            shape(basis.shape, bf16),
            shape((cells, size, size), bf16),
            shape((cells, 1, size), f32),
        ),
        [hbm] * 2,
        [sems] * 3,
    )(*fixed[2:])
    near = joined_exchange(send, slabs, cols, cross)
    x_second, send = call(
        functools.partial(second_body, slab_cells),
        (shape((cells, rows, block), f32), shape((cells, rows, block), bf16)),
        [smem] + [vmem] * (4 + len(near)),
    )(neighbours, rhs, x_first, smoother, tiles, *near)
    near = joined_exchange(send, slabs, cols, cross_now)
    base, send = call(
        functools.partial(third_body, slab_cells),
        (shape((cells, rows, size), f32), shape((cells, 2 * rows, block), bf16)),
        [smem] + [vmem] * (5 + len(near)),
    )(neighbours, rhs, basis, coarse, pivot, tiles, *near)
    near = exchange_apart(send, slabs, cols)
    return call(
        functools.partial(fourth_body, slab_cells),
        (shape((cells, rows, block), f32), shape((cells, rows, size), f32)),
        [smem] + [vmem] * (5 + len(near)),
    )(neighbours, base, x_second, basis, pivot, tiles, *near)


def solution(mesh):
    placed = (
        P(AXES, None, None),
        P(AXES, None, None, None),
        P(AXES, None),
        P(AXES, None, None),
        P(AXES, None, None),
    )
    return jax.shard_map(
        functools.partial(per_device, mesh.shape["slab"], mesh.shape["col"]),
        mesh=mesh,
        in_specs=placed,
        out_specs=(P(AXES, None, None), P(AXES, None, None)),
        check_vma=False,
    )
```

```python
import functools

import jax
import jax.numpy as jnp
from jax import lax
from jax.experimental import pallas as pl
from jax.experimental.pallas import tpu as pltpu
from jax.sharding import PartitionSpec as P

damping = 0.8
AXES = ("slab", "col")
VMEM = pltpu.VMEM
bf16 = jnp.bfloat16
f32 = jnp.float32


def dot(a, b):
    return jnp.dot(a, b, preferred_element_type=f32)


def dot_t(a, b):
    return lax.dot_general(a, b, (((1,), (1,)), ((), ())), preferred_element_type=f32)


def split(value):
    high = value.astype(bf16)
    return high, (value - high.astype(f32)).astype(bf16)


def pairs(slabs, cols, partner):
    groups = []
    for s in range(slabs):
        for c in range(cols):
            s2, c2 = partner(s, c)
            i, j = s * cols + c, (s2 % slabs) * cols + c2
            if i < j:
                groups.append([i, j])
    return groups


def gather(values, slabs, cols, flip):
    return lax.all_gather(
        values,
        AXES,
        axis=0,
        tiled=True,
        axis_index_groups=pairs(slabs, cols, lambda s, c: (s, c ^ flip)),
    )


def crossing(s, c, slabs):
    up = (s % 2 == 0) == (c % 2 == 0)
    return (s + 1 if up else s - 1) % slabs, c ^ 2


def cross(values, slabs, cols):
    def target(s, c):
        s2, c2 = crossing(s, c, slabs)
        return s2 * cols + c2

    return lax.ppermute(
        values,
        AXES,
        [(s * cols + c, target(s, c)) for s in range(slabs) for c in range(cols)],
    )


def cross_now(values, slabs, cols):
    return lax.all_gather(
        values,
        AXES,
        axis=0,
        tiled=True,
        axis_index_groups=pairs(slabs, cols, lambda s, c: crossing(s, c, slabs)),
    )


def merge_body(slabs, cells, beside, out):
    n, extra = cells.shape[0], out.shape[0] - cells.shape[0]
    first = 0
    if beside.shape[0] != extra:
        s, c = lax.axis_index("slab"), lax.axis_index("col")
        up = lax.rem(s, 2) == lax.rem(c, 2)
        other = lax.rem(jnp.where(up, s + 1, s - 1 + slabs), slabs)
        first = jnp.where(s < other, extra, 0)
    for i in range(n):
        out[i] = cells[i]
    for i in range(extra):
        out[n + i] = beside[first + i]


def joined_exchange(cells, slabs, cols, move):
    chip = gather(cells, slabs, cols, 1)
    beside = move(chip, slabs, cols)
    total = (cells.shape[0] + chip.shape[0],) + cells.shape[1:]
    (joined,) = call(
        functools.partial(merge_body, slabs),
        (jax.ShapeDtypeStruct(total, cells.dtype),),
        [pl.BlockSpec(memory_space=VMEM)] * 2,
    )(cells, beside)
    return (lax.all_gather(joined, "col", axis=0, tiled=True),)


def exchange_apart(cells, slabs, cols):
    chip = gather(cells, slabs, cols, 1)
    beside = cross(chip, slabs, cols)
    own = gather(chip, slabs, cols, 2)
    return own, lax.all_gather(beside, "col", axis=0, tiled=True)


def pick(near, cell, here, slab_cells, cells):
    slab = lax.div(cell, slab_cells)
    offset = lax.rem(cell, slab_cells)
    half = slab_cells // 2
    chip, inner = lax.div(offset, half), lax.rem(offset, half)
    odd = jnp.where(lax.div(slab, 2) == lax.div(here, 2), 0, 1)
    col = 2 * (1 - chip) + odd
    if len(near) == 1:
        stride = half + cells
        mine = lax.div(offset, cells) * stride + lax.rem(offset, cells)
        return near[0][jnp.where(slab == here, mine, col * stride + cells + inner)]
    own, halo = near
    return jnp.where(slab == here, own[offset], halo[col * half + inner])


def apply_tiles(near, nb, tiles, slab_cells, first=0):
    here = lax.axis_index("slab")
    cells, kinds = tiles.shape[0], tiles.shape[1]
    sums = [None] * cells
    for t in range(first, kinds):
        for g in range(cells):
            part = dot(pick(near, nb[g, t], here, slab_cells, cells), tiles[g, t])
            sums[g] = part if sums[g] is None else sums[g] + part
    return sums


def load(source, target, sems):
    copies = []
    for g in range(target.shape[0]):
        copies.append(pltpu.make_async_copy(source.at[g], target.at[g], sems.at[g]))
        copies[-1].start()
    return copies


def first_body(smoother_hbm, rhs_hbm, x_out, xb_out, smoother, rhs, smoother_sems, rhs_sems):
    copies = zip(
        load(smoother_hbm, smoother, smoother_sems), load(rhs_hbm, rhs, rhs_sems)
    )
    for g, pair in enumerate(copies):
        for copy in pair:
            copy.wait()
        x = dot(rhs[g].astype(bf16), smoother[g])
        x_out[g] = x
        xb_out[g] = x.astype(bf16)


def coarse_body(
    tiles_hbm, basis_hbm, tiles, basis, coarse_out, pivot_out, own_sems, basis_sems, rest_sems
):
    cells, kinds = tiles.shape[0], tiles.shape[1]
    basis_copies = load(basis_hbm, basis, basis_sems)
    parts = [
        [
            pltpu.make_async_copy(
                tiles_hbm.at[g, pl.ds(first, count)],
                tiles.at[g, pl.ds(first, count)],
                sems.at[g],
            )
            for g in range(cells)
        ]
        for first, count, sems in ((0, 1, own_sems), (1, kinds - 1, rest_sems))
    ]
    for part in parts:
        for copy in part:
            copy.start()
    size = basis.shape[1]
    eye = lax.broadcasted_iota(jnp.int32, (size, size), 0) == lax.broadcasted_iota(
        jnp.int32, (size, size), 1
    )
    for g in range(cells):
        basis_copies[g].wait()
        parts[0][g].wait()
        upper = dot(basis[g], tiles[g, 0]).astype(bf16)
        coarse = dot_t(upper, basis[g]).astype(bf16)
        coarse_out[g] = coarse
        pivot_out[g] = jnp.sum(
            jnp.where(eye, coarse.astype(f32), 0.0), axis=0, keepdims=True
        )
    for copy in parts[1]:
        copy.wait()


def second_body(slab_cells, nb, rhs, x_first, smoother, tiles, *refs):
    *near, x_out, xb_out = refs
    sums = apply_tiles(near, nb, tiles, slab_cells)
    steps = [
        dot((rhs[g] - image).astype(bf16), smoother[g]) for g, image in enumerate(sums)
    ]
    for g, step in enumerate(steps):
        x = x_first[g] + step
        x_out[g] = x
        xb_out[g] = x.astype(bf16)


def third_body(
    slab_cells, nb, rhs, basis, coarse, pivot, tiles, *refs
):
    *near, base_out, fine_out = refs
    sums = apply_tiles(near, nb, tiles, slab_cells)
    rows = rhs.shape[1]
    every = range(len(sums))
    coarse_rhs = [dot_t((rhs[g] - sums[g]).astype(bf16), basis[g]) for g in every]
    c_first = [damping * coarse_rhs[g] / pivot[g] for g in every]
    rounded = [c.astype(bf16) for c in c_first]
    fine = [dot(rounded[g], basis[g]) for g in every]
    own = [dot(rounded[g], coarse[g]) for g in every]
    for g in every:
        high, low = split(fine[g])
        fine_out[g, :rows] = high
        fine_out[g, rows:] = low
        base_out[g] = c_first[g] + damping * (coarse_rhs[g] - own[g]) / pivot[g]


def fourth_body(
    slab_cells, nb, base, x_second, basis, pivot, tiles, *refs
):
    *near, sol_out, iter_out = refs
    sums = apply_tiles(near, nb, tiles, slab_cells, 1)
    rows = x_second.shape[1]
    every = range(len(sums))
    parts = [jnp.concatenate(split(sums[g][:rows] + sums[g][rows:])) for g in every]
    both = [dot_t(parts[g], basis[g]) for g in every]
    iterates = [base[g] - damping * (both[g][:rows] + both[g][rows:]) / pivot[g] for g in every]
    steps = [dot(iterates[g].astype(bf16), basis[g]) for g in every]
    for g in every:
        iter_out[g] = iterates[g]
        sol_out[g] = x_second[g] + steps[g]


def call(body, outs, specs, scratch=(), limit=24 * 2**20, moved=None):
    return pl.pallas_call(
        body,
        out_shape=outs,
        in_specs=specs,
        out_specs=tuple(pl.BlockSpec(memory_space=VMEM) for _ in outs),
        scratch_shapes=list(scratch),
        compiler_params=pltpu.CompilerParams(vmem_limit_bytes=limit),
        cost_estimate=moved
        and pl.CostEstimate(flops=0, transcendentals=0, bytes_accessed=moved),
    )


def per_device(slabs, cols, rhs, tiles, neighbours, smoother, basis):
    cells, rows, block = rhs.shape
    size = basis.shape[1]
    slab_cells = cells * cols
    shape = jax.ShapeDtypeStruct
    vmem = pl.BlockSpec(memory_space=VMEM)
    hbm = pl.BlockSpec(memory_space=pltpu.HBM)
    smem = pl.BlockSpec(memory_space=pltpu.SMEM)
    fixed = [
        pltpu.with_memory_space_constraint(v, pltpu.HBM) for v in (smoother, rhs, tiles, basis)
    ]
    sems = pltpu.SemaphoreType.DMA((cells,))
    x_first, send, smoother, rhs = call(
        first_body,
        (
            shape((cells, rows, block), f32),
            shape((cells, rows, block), bf16),
            shape(smoother.shape, bf16),
            shape(rhs.shape, f32),
        ),
        [hbm] * 2,
        [sems] * 2,
    )(*fixed[:2])
    tiles, basis, coarse, pivot = call(
        coarse_body,
        (
            shape(tiles.shape, bf16),
            shape(basis.shape, bf16),
            shape((cells, size, size), bf16),
            shape((cells, 1, size), f32),
        ),
        [hbm] * 2,
        [sems] * 3,
    )(*fixed[2:])
    near = joined_exchange(send, slabs, cols, cross)
    x_second, send = call(
        functools.partial(second_body, slab_cells),
        (shape((cells, rows, block), f32), shape((cells, rows, block), bf16)),
        [smem] + [vmem] * (4 + len(near)),
    )(neighbours, rhs, x_first, smoother, tiles, *near)
    near = joined_exchange(send, slabs, cols, cross_now)
    base, send = call(
        functools.partial(third_body, slab_cells),
        (shape((cells, rows, size), f32), shape((cells, 2 * rows, block), bf16)),
        [smem] + [vmem] * (5 + len(near)),
    )(neighbours, rhs, basis, coarse, pivot, tiles, *near)
    near = exchange_apart(send, slabs, cols)
    return call(
        functools.partial(fourth_body, slab_cells),
        (shape((cells, rows, block), f32), shape((cells, rows, size), f32)),
        [smem] + [vmem] * (5 + len(near)),
    )(neighbours, base, x_second, basis, pivot, tiles, *near)


def solution(mesh):
    placed = (
        P(AXES, None, None),
        P(AXES, None, None, None),
        P(AXES, None),
        P(AXES, None, None),
        P(AXES, None, None),
    )
    return jax.shard_map(
        functools.partial(per_device, mesh.shape["slab"], mesh.shape["col"]),
        mesh=mesh,
        in_specs=placed,
        out_specs=(P(AXES, None, None), P(AXES, None, None)),
        check_vma=False,
    )
```

```python
import functools

import jax
import jax.numpy as jnp
from jax import lax
from jax.experimental import pallas as pl
from jax.experimental.pallas import tpu as pltpu
from jax.sharding import PartitionSpec as P

damping = 0.8
AXES = ("slab", "col")
VMEM = pltpu.VMEM
bf16 = jnp.bfloat16
f32 = jnp.float32


def dot(a, b):
    return jnp.dot(a, b, preferred_element_type=f32)


def dot_t(a, b):
    return lax.dot_general(a, b, (((1,), (1,)), ((), ())), preferred_element_type=f32)


def split(value):
    high = value.astype(bf16)
    return high, (value - high.astype(f32)).astype(bf16)


def pairs(slabs, cols, partner):
    groups = []
    for s in range(slabs):
        for c in range(cols):
            s2, c2 = partner(s, c)
            i, j = s * cols + c, (s2 % slabs) * cols + c2
            if i < j:
                groups.append([i, j])
    return groups


def gather(values, slabs, cols, flip):
    return lax.all_gather(
        values,
        AXES,
        axis=0,
        tiled=True,
        axis_index_groups=pairs(slabs, cols, lambda s, c: (s, c ^ flip)),
    )


def crossing(s, c, slabs):
    up = (s % 2 == 0) == (c % 2 == 0)
    return (s + 1 if up else s - 1) % slabs, c ^ 2


def cross(values, slabs, cols):
    def target(s, c):
        s2, c2 = crossing(s, c, slabs)
        return s2 * cols + c2

    return lax.ppermute(
        values,
        AXES,
        [(s * cols + c, target(s, c)) for s in range(slabs) for c in range(cols)],
    )


def cross_now(values, slabs, cols):
    return lax.all_gather(
        values,
        AXES,
        axis=0,
        tiled=True,
        axis_index_groups=pairs(slabs, cols, lambda s, c: crossing(s, c, slabs)),
    )


def merge_body(slabs, cells, beside, out):
    n, extra = cells.shape[0], out.shape[0] - cells.shape[0]
    first = 0
    if beside.shape[0] != extra:
        s, c = lax.axis_index("slab"), lax.axis_index("col")
        up = lax.rem(s, 2) == lax.rem(c, 2)
        other = lax.rem(jnp.where(up, s + 1, s - 1 + slabs), slabs)
        first = jnp.where(s < other, extra, 0)
    for i in range(n):
        out[i] = cells[i]
    for i in range(extra):
        out[n + i] = beside[first + i]


def joined_exchange(cells, slabs, cols, move):
    chip = gather(cells, slabs, cols, 1)
    beside = move(chip, slabs, cols)
    total = (cells.shape[0] + chip.shape[0],) + cells.shape[1:]
    (joined,) = call(
        functools.partial(merge_body, slabs),
        (jax.ShapeDtypeStruct(total, cells.dtype),),
        [pl.BlockSpec(memory_space=VMEM)] * 2,
    )(cells, beside)
    return (lax.all_gather(joined, "col", axis=0, tiled=True),)


def exchange_apart(cells, slabs, cols):
    chip = gather(cells, slabs, cols, 1)
    beside = cross(chip, slabs, cols)
    own = gather(chip, slabs, cols, 2)
    return own, lax.all_gather(beside, "col", axis=0, tiled=True)


def pick(near, cell, here, slab_cells, cells):
    slab = lax.div(cell, slab_cells)
    offset = lax.rem(cell, slab_cells)
    half = slab_cells // 2
    chip, inner = lax.div(offset, half), lax.rem(offset, half)
    odd = jnp.where(lax.div(slab, 2) == lax.div(here, 2), 0, 1)
    col = 2 * (1 - chip) + odd
    if len(near) == 1:
        stride = half + cells
        mine = lax.div(offset, cells) * stride + lax.rem(offset, cells)
        return near[0][jnp.where(slab == here, mine, col * stride + cells + inner)]
    own, halo = near
    return jnp.where(slab == here, own[offset], halo[col * half + inner])


def apply_tiles(near, nb, tiles, slab_cells, first=0):
    here = lax.axis_index("slab")
    cells, kinds = tiles.shape[0], tiles.shape[1]
    sums = [None] * cells
    for t in range(first, kinds):
        for g in range(cells):
            part = dot(pick(near, nb[g, t], here, slab_cells, cells), tiles[g, t])
            sums[g] = part if sums[g] is None else sums[g] + part
    return sums


def load(source, target, sems):
    copies = []
    for g in range(target.shape[0]):
        copies.append(pltpu.make_async_copy(source.at[g], target.at[g], sems.at[g]))
        copies[-1].start()
    return copies


def first_body(smoother_hbm, rhs_hbm, x_out, xb_out, smoother, rhs, smoother_sems, rhs_sems):
    copies = zip(
        load(smoother_hbm, smoother, smoother_sems), load(rhs_hbm, rhs, rhs_sems)
    )
    for g, pair in enumerate(copies):
        for copy in pair:
            copy.wait()
        x = dot(rhs[g].astype(bf16), smoother[g])
        x_out[g] = x
        xb_out[g] = x.astype(bf16)


def coarse_body(
    tiles_hbm, basis_hbm, tiles, basis, coarse_out, pivot_out, own_sems, basis_sems, rest_sems
):
    cells, kinds = tiles.shape[0], tiles.shape[1]
    basis_copies = load(basis_hbm, basis, basis_sems)
    parts = [
        [
            pltpu.make_async_copy(
                tiles_hbm.at[g, pl.ds(first, count)],
                tiles.at[g, pl.ds(first, count)],
                sems.at[g],
            )
            for g in range(cells)
        ]
        for first, count, sems in ((0, 1, own_sems), (1, kinds - 1, rest_sems))
    ]
    for part in parts:
        for copy in part:
            copy.start()
    size = basis.shape[1]
    eye = lax.broadcasted_iota(jnp.int32, (size, size), 0) == lax.broadcasted_iota(
        jnp.int32, (size, size), 1
    )
    for g in range(cells):
        basis_copies[g].wait()
        parts[0][g].wait()
        upper = dot(basis[g], tiles[g, 0]).astype(bf16)
        coarse = dot_t(upper, basis[g]).astype(bf16)
        coarse_out[g] = coarse
        pivot_out[g] = jnp.sum(
            jnp.where(eye, coarse.astype(f32), 0.0), axis=0, keepdims=True
        )
    for copy in parts[1]:
        copy.wait()


def second_body(slab_cells, nb, rhs, x_first, smoother, tiles, *refs):
    *near, x_out, xb_out = refs
    sums = apply_tiles(near, nb, tiles, slab_cells)
    steps = [
        dot((rhs[g] - image).astype(bf16), smoother[g]) for g, image in enumerate(sums)
    ]
    for g, step in enumerate(steps):
        x = x_first[g] + step
        x_out[g] = x
        xb_out[g] = x.astype(bf16)


def third_body(
    slab_cells, nb, rhs, basis, coarse, pivot, tiles, *refs
):
    *near, base_out, fine_out = refs
    sums = apply_tiles(near, nb, tiles, slab_cells)
    rows = rhs.shape[1]
    every = range(len(sums))
    coarse_rhs = [dot_t((rhs[g] - sums[g]).astype(bf16), basis[g]) for g in every]
    c_first = [damping * coarse_rhs[g] / pivot[g] for g in every]
    rounded = [c.astype(bf16) for c in c_first]
    fine = [dot(rounded[g], basis[g]) for g in every]
    own = [dot(rounded[g], coarse[g]) for g in every]
    for g in every:
        high, low = split(fine[g])
        fine_out[g, :rows] = high
        fine_out[g, rows:] = low
        base_out[g] = c_first[g] + damping * (coarse_rhs[g] - own[g]) / pivot[g]


def fourth_body(
    slab_cells, nb, base, x_second, basis, pivot, tiles, *refs
):
    *near, sol_out, iter_out = refs
    sums = apply_tiles(near, nb, tiles, slab_cells, 1)
    rows = x_second.shape[1]
    every = range(len(sums))
    parts = [jnp.concatenate(split(sums[g][:rows] + sums[g][rows:])) for g in every]
    both = [dot_t(parts[g], basis[g]) for g in every]
    iterates = [base[g] - damping * (both[g][:rows] + both[g][rows:]) / pivot[g] for g in every]
    steps = [dot(iterates[g].astype(bf16), basis[g]) for g in every]
    for g in every:
        iter_out[g] = iterates[g]
        sol_out[g] = x_second[g] + steps[g]


def call(body, outs, specs, scratch=(), limit=24 * 2**20, moved=None):
    return pl.pallas_call(
        body,
        out_shape=outs,
        in_specs=specs,
        out_specs=tuple(pl.BlockSpec(memory_space=VMEM) for _ in outs),
        scratch_shapes=list(scratch),
        compiler_params=pltpu.CompilerParams(vmem_limit_bytes=limit),
        cost_estimate=moved
        and pl.CostEstimate(flops=0, transcendentals=0, bytes_accessed=moved),
    )


def per_device(slabs, cols, rhs, tiles, neighbours, smoother, basis):
    cells, rows, block = rhs.shape
    size = basis.shape[1]
    slab_cells = cells * cols
    shape = jax.ShapeDtypeStruct
    vmem = pl.BlockSpec(memory_space=VMEM)
    hbm = pl.BlockSpec(memory_space=pltpu.HBM)
    smem = pl.BlockSpec(memory_space=pltpu.SMEM)
    fixed = [
        pltpu.with_memory_space_constraint(v, pltpu.HBM) for v in (smoother, rhs, tiles, basis)
    ]
    sems = pltpu.SemaphoreType.DMA((cells,))
    x_first, send, smoother, rhs = call(
        first_body,
        (
            shape((cells, rows, block), f32),
            shape((cells, rows, block), bf16),
            shape(smoother.shape, bf16),
            shape(rhs.shape, f32),
        ),
        [hbm] * 2,
        [sems] * 2,
    )(*fixed[:2])
    tiles, basis, coarse, pivot = call(
        coarse_body,
        (
            shape(tiles.shape, bf16),
            shape(basis.shape, bf16),
            shape((cells, size, size), bf16),
            shape((cells, 1, size), f32),
        ),
        [hbm] * 2,
        [sems] * 3,
    )(*fixed[2:])
    near = joined_exchange(send, slabs, cols, cross)
    x_second, send = call(
        functools.partial(second_body, slab_cells),
        (shape((cells, rows, block), f32), shape((cells, rows, block), bf16)),
        [smem] + [vmem] * (4 + len(near)),
    )(neighbours, rhs, x_first, smoother, tiles, *near)
    near = exchange_apart(send, slabs, cols)
    base, send = call(
        functools.partial(third_body, slab_cells),
        (shape((cells, rows, size), f32), shape((cells, 2 * rows, block), bf16)),
        [smem] + [vmem] * (5 + len(near)),
    )(neighbours, rhs, basis, coarse, pivot, tiles, *near)
    near = exchange_apart(send, slabs, cols)
    return call(
        functools.partial(fourth_body, slab_cells),
        (shape((cells, rows, block), f32), shape((cells, rows, size), f32)),
        [smem] + [vmem] * (5 + len(near)),
    )(neighbours, base, x_second, basis, pivot, tiles, *near)


def solution(mesh):
    placed = (
        P(AXES, None, None),
        P(AXES, None, None, None),
        P(AXES, None),
        P(AXES, None, None),
        P(AXES, None, None),
    )
    return jax.shard_map(
        functools.partial(per_device, mesh.shape["slab"], mesh.shape["col"]),
        mesh=mesh,
        in_specs=placed,
        out_specs=(P(AXES, None, None), P(AXES, None, None)),
        check_vma=False,
    )
```
